32 devices in a mesh: dp: 16 (over z, x, core), ctx: 2 (over y).
Axes of the slice: x: 2, y: 2, z: 4, core: 2. Of those that a mesh axis runs over, the one named last changes fastest.
Arguments:
- block_in: bfloat16 [16, 256, 1088], P('dp', 'ctx'), may hold values from -6 to 6
- cotangent: bfloat16 [16, 256, 1088], P('dp', 'ctx'), may hold values from -6 to 6
- block_order: int32 [4], replicated, may hold values from 0 to 3, each once
- ln1_gain: bfloat16 [1088], P('dp'), may hold values from 0.25 to 1.75
- ln1_bias: bfloat16 [1088], P('dp'), may hold values from -2 to 2
- w_qkv: bfloat16 [1088, 3264], P('dp'), may hold values from -1 to 1
- b_query: bfloat16 [1088], P('dp'), may hold values from -2 to 2
- b_value: bfloat16 [1088], P('dp'), may hold values from -2 to 2
- w_out: bfloat16 [1088, 1088], P('dp'), may hold values from -1 to 1
- b_out: bfloat16 [1088], P('dp'), may hold values from -2 to 2
- ln2_gain: bfloat16 [1088], P('dp'), may hold values from 0.25 to 1.75
- ln2_bias: bfloat16 [1088], P('dp'), may hold values from -2 to 2
- w_up: bfloat16 [1088, 4352], P(None, 'dp'), may hold values from -0.1875 to 0.1875
- b_up: bfloat16 [4352], P('dp'), may hold values from -2 to 2
- w_down: bfloat16 [4352, 1088], P('dp'), may hold values from -0.09375 to 0.09375
- b_down: bfloat16 [1088], P('dp'), may hold values from -2 to 2
Outputs:
- block_out: bfloat16 [16, 256, 1088], P('dp', 'ctx')
- input_grad: float32 [16, 256, 1088], P('dp', 'ctx')
- g_ln1_gain: float32 [1088], P('dp')
- g_ln1_bias: float32 [1088], P('dp')
- g_w_qkv: float32 [1088, 3264], P('dp', 'ctx')
- g_b_query: float32 [1088], P('dp')
- g_b_value: float32 [1088], P('dp')
- g_w_out: float32 [1088, 1088], P('dp', 'ctx')
- g_b_out: float32 [1088], P('dp')
- g_ln2_gain: float32 [1088], P('dp')
- g_ln2_bias: float32 [1088], P('dp')
- g_w_up: float32 [1088, 4352], P('ctx', 'dp')
- g_b_up: float32 [4352], P('dp')
- g_w_down: float32 [4352, 1088], P('dp', 'ctx')
- g_b_down: float32 [1088], P('dp')
The draws below stay inside these ranges and needn't reach their ends.
Inputs may be any that keep to these rules, and one draw needn't show every extreme that they name: `block_order`: each block number appears once.
All inputs are finite; a program needn't handle non-finite values.
Results may differ from the reference program's by a relative error of at most 0.011.
Values may be sent and summed in bfloat16 or wider, within the bound.
A program may use at most 192 MiB of HBM per device.

```python
import math
import jax
import jax.numpy as jnp
from jax import lax

D = 1088
HEADS = 17
HD = 64
FF = 4352
BL = 64
SEQS = 16
BLOCKS = 4
SEQ = 256


def draw_w_qkv(key, part):
    scale = 1.0 / math.sqrt(D)
    drawn = jax.random.normal(jax.random.fold_in(key, 1), (D, 3 * D), jnp.float32) * scale
    return jnp.clip(drawn, -0.99, 0.99).astype(jnp.bfloat16)


def steps_of(stream_key, extent, cuts, smallest, high):
    loudness = 1.0
    for position, shards_of in cuts:
        steps = jax.random.uniform(jax.random.fold_in(jax.random.fold_in(stream_key, 6), position), (shards_of,), jnp.float32, smallest / len(cuts), high / len(cuts))
        loudness = loudness * jnp.repeat(jnp.exp(steps), extent[position] // shards_of).reshape((-1,) + (1,) * (len(extent) - 1 - position))
    return loudness


def scatter_about(rng, dims, width, reach, shards=(), held_as=jnp.bfloat16):
    values = jax.random.normal(rng, dims, jnp.float32) * width
    if len(shards) > 0:
        values = steps_of(rng, dims, shards, -0.22, 0.18) * values
    return jnp.clip(values, min=-reach, max=reach).astype(held_as)


def setup_inputs(seed: int = 0) -> dict:
    keys = jax.random.split(jax.random.key(seed), 17)
    block_in = scatter_about(keys[0], (SEQS, SEQ, D), 1.0, 6.0, ((0, 16), (1, 2)))
    cotangent = scatter_about(keys[1], (SEQS, SEQ, D), 1.0, 6.0, ((0, 16), (1, 2)))
    block_order = jax.random.permutation(keys[2], BLOCKS).astype(jnp.int32)
    ln1_gain = jnp.clip(1.0 + 0.15 * jax.random.normal(keys[3], (D,), jnp.float32), 0.25, 1.75).astype(jnp.bfloat16)
    ln1_bias = scatter_about(keys[4], (D,), 0.3, 2.0, ((0, 16),))
    w_qkv = draw_w_qkv(jax.random.fold_in(keys[16], 71), 0)
    b_query = scatter_about(keys[6], (D,), 0.3, 2.0, ((0, 16),))
    b_value = scatter_about(keys[7], (D,), 0.3, 2.0, ((0, 16),))
    w_out = scatter_about(keys[8], (D, D), (D // 32) ** -0.5, 1.0, ((0, 16),))
    b_out = scatter_about(keys[9], (D,), 0.3, 2.0, ((0, 16),))
    ln2_gain = jnp.clip(1.0 + 0.15 * jax.random.normal(keys[10], (D,), jnp.float32), 0.25, 1.75).astype(jnp.bfloat16)
    ln2_bias = scatter_about(keys[11], (D,), 0.3, 2.0, ((0, 16),))
    w_up = scatter_about(keys[12], (D, FF), D ** -0.5, 0.1875, ((1, 16),))
    b_up = scatter_about(keys[13], (FF,), 0.3, 2.0, ((0, 16),))
    w_down = scatter_about(keys[14], (FF, D), FF ** -0.5, 0.09375, ((0, 16),))
    b_down = scatter_about(keys[15], (D,), 0.3, 2.0, ((0, 16),))
    return {"block_in": block_in, "cotangent": cotangent, "block_order": block_order, "ln1_gain": ln1_gain, "ln1_bias": ln1_bias, "w_qkv": w_qkv, "b_query": b_query, "b_value": b_value, "w_out": w_out, "b_out": b_out, "ln2_gain": ln2_gain, "ln2_bias": ln2_bias, "w_up": w_up, "b_up": b_up, "w_down": w_down, "b_down": b_down}


def rounded(values):
    return lax.optimization_barrier(values.astype(jnp.bfloat16))

def norm_parts(values, gain_values, shift_values):
    average = lax.optimization_barrier(jnp.mean(values, axis=-1, keepdims=True))
    centered = values - average
    inverse = lax.rsqrt(lax.optimization_barrier(jnp.mean(centered * centered, axis=-1, keepdims=True)) + 1e-05)
    normed = centered * inverse
    return (normed * gain_values.astype(jnp.float32) + shift_values.astype(jnp.float32), normed, inverse)

def norm_back(upstream, normed, inverse, gain_values):
    scaled = upstream * gain_values.astype(jnp.float32)
    return inverse * (scaled - lax.optimization_barrier(jnp.mean(scaled, axis=-1, keepdims=True)) - normed * lax.optimization_barrier(jnp.mean(scaled * normed, axis=-1, keepdims=True)))

def gelu_slope(values):
    return 0.5 * (1.0 + lax.erf(values * 0.7071067811865476)) + values * jnp.exp(-0.5 * values * values) * 0.3989422804014327

def sequence_pass(inputs, upstream_b, positions, params):
    ln1_gain, ln1_bias, w_qkv, b_query, b_value, w_out, b_out, ln2_gain, ln2_bias, w_up, b_up, w_down, b_down = params
    length = inputs.shape[0]
    residual = inputs.astype(jnp.float32)
    normed_in_f, normed_one, inverse_one = norm_parts(residual, ln1_gain, ln1_bias)
    normed_in = rounded(normed_in_f)
    projected = jnp.dot(normed_in, w_qkv, preferred_element_type=jnp.float32)
    queries = rounded(projected[:, :D] + b_query.astype(jnp.float32))
    key_rows = rounded(projected[:, D:2 * D])
    value_rows = rounded(projected[:, 2 * D:] + b_value.astype(jnp.float32))
    query_f = queries.astype(jnp.float32).reshape(length, HEADS, HD)
    key_f = key_rows.astype(jnp.float32).reshape(length, HEADS, HD)
    value_f = value_rows.astype(jnp.float32).reshape(length, HEADS, HD)
    allowed = positions[:, None] >= positions[None, :]
    scores = jnp.where(allowed, jnp.einsum('qhd,khd->hqk', query_f, key_f) * 0.125, -1e+30)
    largest = lax.optimization_barrier(jnp.max(scores, axis=-1, keepdims=True))
    exponent = jnp.where(allowed, jnp.exp(scores - largest), 0.0)
    totals = lax.optimization_barrier(jnp.sum(exponent, axis=-1, keepdims=True))
    logsum = largest + jnp.log(totals)
    context = jnp.einsum('hqk,khd->qhd', exponent / totals, value_f, precision=lax.Precision.HIGHEST)
    attended = rounded(context.reshape(length, D))
    hidden_one = residual + jnp.dot(attended, w_out, preferred_element_type=jnp.float32) + b_out.astype(jnp.float32)
    normed_mid_f, normed_two, inverse_two = norm_parts(hidden_one, ln2_gain, ln2_bias)
    normed_mid = rounded(normed_mid_f)
    pre_act = jnp.dot(normed_mid, w_up, preferred_element_type=jnp.float32) + b_up.astype(jnp.float32)
    activated = rounded(jax.nn.gelu(pre_act, approximate=False))
    block_out = (hidden_one + jnp.dot(activated, w_down, preferred_element_type=jnp.float32) + b_down.astype(jnp.float32)).astype(jnp.bfloat16)
    upstream = upstream_b.astype(jnp.float32)
    grad_down = jnp.dot(activated.T, upstream_b, preferred_element_type=jnp.float32)
    grad_pre = jnp.dot(upstream_b, w_down.T, preferred_element_type=jnp.float32) * gelu_slope(pre_act)
    grad_pre_b = rounded(grad_pre)
    grad_up = jnp.dot(normed_mid.T, grad_pre_b, preferred_element_type=jnp.float32)
    grad_mid = jnp.dot(grad_pre_b, w_up.T, preferred_element_type=jnp.float32)
    grad_hidden = upstream + norm_back(grad_mid, normed_two, inverse_two, ln2_gain)
    grad_hidden_b = rounded(grad_hidden)
    grad_out_w = jnp.dot(attended.T, grad_hidden_b, preferred_element_type=jnp.float32)
    grad_context = rounded(jnp.dot(grad_hidden_b, w_out.T, preferred_element_type=jnp.float32))
    grad_ctx_f = grad_context.astype(jnp.float32).reshape(length, HEADS, HD)
    attended_f = attended.astype(jnp.float32).reshape(length, HEADS, HD)
    row_delta = jnp.einsum('qhd,qhd->hq', grad_ctx_f, attended_f)
    probability = jnp.where(allowed, jnp.exp(scores - logsum), 0.0)
    prob_b = rounded(probability).astype(jnp.float32)
    grad_value = jnp.einsum('hqk,qhd->khd', prob_b, grad_ctx_f)
    grad_prob = jnp.einsum('qhd,khd->hqk', grad_ctx_f, value_f)
    grad_score = rounded(probability * (grad_prob - row_delta[:, :, None])).astype(jnp.float32)
    grad_query = jnp.einsum('hqk,khd->qhd', grad_score, key_f) * 0.125
    grad_key = jnp.einsum('hqk,qhd->khd', grad_score, query_f) * 0.125
    grad_qkv = rounded(jnp.concatenate([grad_query.reshape(length, D), grad_key.reshape(length, D), grad_value.reshape(length, D)], axis=1))
    grad_qkv_w = jnp.dot(normed_in.T, grad_qkv, preferred_element_type=jnp.float32)
    grad_in_norm = jnp.dot(grad_qkv, w_qkv.T, preferred_element_type=jnp.float32)
    grad_input = grad_hidden + norm_back(grad_in_norm, normed_one, inverse_one, ln1_gain)
    grads = (lax.optimization_barrier(jnp.sum(grad_in_norm * normed_one, axis=0)), lax.optimization_barrier(jnp.sum(grad_in_norm, axis=0)), grad_qkv_w, lax.optimization_barrier(jnp.sum(grad_query, axis=0)).reshape(D), lax.optimization_barrier(jnp.sum(grad_value, axis=0)).reshape(D), grad_out_w, lax.optimization_barrier(jnp.sum(grad_hidden, axis=0)), lax.optimization_barrier(jnp.sum(grad_mid * normed_two, axis=0)), lax.optimization_barrier(jnp.sum(grad_mid, axis=0)), grad_up, lax.optimization_barrier(jnp.sum(grad_pre, axis=0)), grad_down, lax.optimization_barrier(jnp.sum(upstream, axis=0)))
    return (block_out, grad_input, grads)

def reference(block_in, cotangent, block_order, ln1_gain, ln1_bias, w_qkv, b_query, b_value, w_out, b_out, ln2_gain, ln2_bias, w_up, b_up, w_down, b_down):
    params = (ln1_gain, ln1_bias, w_qkv, b_query, b_value, w_out, b_out, ln2_gain, ln2_bias, w_up, b_up, w_down, b_down)
    slot_index = jnp.arange(SEQ, dtype=jnp.int32)
    positions = (block_order[slot_index // BL] * BL + slot_index % BL).astype(jnp.int32)
    empty_grads = tuple((jnp.zeros(member.shape, jnp.float32) for member in params))

    def visit(running, sequence_pair):
        out_rows, grad_rows, grads = sequence_pass(sequence_pair[0], sequence_pair[1], positions, params)
        return (tuple((left + right for left, right in zip(running, grads))), (out_rows, grad_rows))
    totals, outputs = lax.scan(visit, empty_grads, (block_in, cotangent))
    return (outputs[0], outputs[1], totals[0], totals[1], totals[2], totals[3], totals[4], totals[5], totals[6], totals[7], totals[8], totals[9], totals[10], totals[11], totals[12])
```

```python
import functools

import jax
import jax.numpy as jnp
from jax import lax
from jax.experimental import pallas as pl
from jax.experimental.pallas import tpu as pltpu
from jax.sharding import PartitionSpec as P

HD = 64
SCALE = 0.125


def norm_parts(values, gain_values, shift_values):
    average = jnp.mean(values, axis=-1, keepdims=True)
    centered = values - average
    inverse = lax.rsqrt(jnp.mean(centered * centered, axis=-1, keepdims=True) + 1e-05)
    normed = centered * inverse
    return normed * gain_values + shift_values, normed, inverse


def norm_back(upstream, normed, inverse, gain_values):
    scaled = upstream * gain_values
    return inverse * (
        scaled
        - jnp.mean(scaled, axis=-1, keepdims=True)
        - normed * jnp.mean(scaled * normed, axis=-1, keepdims=True)
    )


def gelu_slope(values):
    return (
        0.5 * (1.0 + lax.erf(values * 0.7071067811865476))
        + values * jnp.exp(-0.5 * values * values) * 0.3989422804014327
    )


def contract_first(left, right):
    return lax.dot_general(
        left, right, (((0,), (0,)), ((), ())), preferred_element_type=jnp.float32
    )


def contract_last(left, right):
    return lax.dot_general(
        left, right, (((1,), (1,)), ((), ())), preferred_element_type=jnp.float32
    )


def head_groups(width):
    groups = [(start, 128) for start in range(0, width - width % 128, 128)]
    if width % 128:
        groups.append((width - width % 128, width % 128))
    return groups


def head_masks(lanes):
    if lanes == HD:
        return [None]
    lane = lax.broadcasted_iota(jnp.int32, (1, lanes), 1)
    return [
        jnp.where((lane >= first) & (lane < first + HD), 1.0, 0.0).astype(jnp.bfloat16)
        for first in range(0, lanes, HD)
    ]


def keep(array, mask):
    return array if mask is None else array * mask


def visible_bias(query_pos_ref, key_pos_ref):
    return jnp.where(query_pos_ref[...] >= key_pos_ref[...], 0.0, -1e30)


def attend_kernel(query_pos_ref, key_pos_ref, q_ref, k_ref, v_ref, o_ref):
    bias = visible_bias(query_pos_ref, key_pos_ref)
    for start, lanes in head_groups(q_ref.shape[1]):
        block = slice(start, start + lanes)
        q, k, v = q_ref[:, block], k_ref[:, block], v_ref[:, block]
        total = None
        for mask in head_masks(lanes):
            scores = contract_last(keep(q, mask), k) * SCALE + bias
            largest = jnp.max(scores, axis=-1, keepdims=True)
            exponent = jnp.exp(scores - largest)
            inverse = 1.0 / jnp.sum(exponent, axis=-1, keepdims=True)
            part = (
                jnp.dot(
                    exponent.astype(jnp.bfloat16),
                    keep(v, mask),
                    preferred_element_type=jnp.float32,
                )
                * inverse
            )
            total = part if total is None else total + part
        o_ref[:, block] = total.astype(o_ref.dtype)


def attend_back_kernel(
    query_pos_ref,
    key_pos_ref,
    q_ref,
    k_ref,
    v_ref,
    do_ref,
    o_ref,
    dq_ref,
    dk_ref,
    dv_ref,
    dq_sum_ref,
    dv_sum_ref,
):
    bias = visible_bias(query_pos_ref, key_pos_ref)
    for start, lanes in head_groups(q_ref.shape[1]):
        block = slice(start, start + lanes)
        q, k, v = q_ref[:, block], k_ref[:, block], v_ref[:, block]
        do, o = do_ref[:, block], o_ref[:, block]
        product = do.astype(jnp.float32) * o.astype(jnp.float32)
        dq = dk = dv = None
        for mask in head_masks(lanes):
            q_h, k_h, do_h = keep(q, mask), keep(k, mask), keep(do, mask)
            product_h = product if mask is None else product * mask.astype(jnp.float32)
            delta = jnp.sum(product_h, axis=-1, keepdims=True)
            scores = contract_last(q_h, k) * SCALE + bias
            largest = jnp.max(scores, axis=-1, keepdims=True)
            exponent = jnp.exp(scores - largest)
            p = exponent * (1.0 / jnp.sum(exponent, axis=-1, keepdims=True))
            dp = contract_last(do_h, v)
            ds = (p * (dp - delta)).astype(jnp.bfloat16)
            dv_h = contract_first(p.astype(jnp.bfloat16), do_h)
            dq_h = jnp.dot(ds, k_h, preferred_element_type=jnp.float32)
            dk_h = contract_first(ds, q_h)
            dq = dq_h if dq is None else dq + dq_h
            dk = dk_h if dk is None else dk + dk_h
            dv = dv_h if dv is None else dv + dv_h
        dq = dq * SCALE
        dq_ref[:, block] = dq.astype(dq_ref.dtype)
        dk_ref[:, block] = (dk * SCALE).astype(dk_ref.dtype)
        dv_ref[:, block] = dv.astype(dv_ref.dtype)
        dq_sum_ref[:, block] = jnp.sum(dq, axis=0, keepdims=True)
        dv_sum_ref[:, block] = jnp.sum(dv, axis=0, keepdims=True)


def whole_vmem(count):
    return [pl.BlockSpec(memory_space=pltpu.VMEM)] * count


def attend(query_pos, key_pos, q, k, v):
    rows, width = q.shape
    keys = k.shape[0]
    return pl.pallas_call(
        attend_kernel,
        out_shape=jax.ShapeDtypeStruct((rows, width), jnp.bfloat16),
        in_specs=whole_vmem(5),
        out_specs=pl.BlockSpec(memory_space=pltpu.VMEM),
        cost_estimate=pl.CostEstimate(
            flops=8 * rows * keys * width,
            bytes_accessed=4 * (rows + keys) * width,
            transcendentals=rows * keys * (width // HD),
        ),
    )(query_pos, key_pos, q, k, v)


def attend_back(query_pos, key_pos, q, k, v, do, o):
    rows, width = q.shape
    keys = k.shape[0]
    return pl.pallas_call(
        attend_back_kernel,
        out_shape=(
            jax.ShapeDtypeStruct((rows, width), jnp.bfloat16),
            jax.ShapeDtypeStruct((keys, width), jnp.bfloat16),
            jax.ShapeDtypeStruct((keys, width), jnp.bfloat16),
            jax.ShapeDtypeStruct((1, width), jnp.float32),
            jax.ShapeDtypeStruct((1, width), jnp.float32),
        ),
        in_specs=whole_vmem(7),
        out_specs=tuple(whole_vmem(5)),
        cost_estimate=pl.CostEstimate(
            flops=20 * rows * keys * width,
            bytes_accessed=8 * (rows + keys) * width,
            transcendentals=rows * keys * (width // HD),
        ),
    )(query_pos, key_pos, q, k, v, do, o)


def shift(array, axis, by):
    peers = lax.axis_size(axis)
    return lax.ppermute(array, axis, [(i, (i + by) % peers) for i in range(peers)])


def gather_direct(array, axis):
    peers = lax.axis_size(axis)
    mine = lax.axis_index(axis)
    held = [array] + [shift(array, axis, by) for by in range(1, peers)]
    stacked = jnp.zeros((peers,) + array.shape, array.dtype)
    for by in range(peers):
        stacked = lax.dynamic_update_index_in_dim(stacked, held[by], (mine - by) % peers, 0)
    return stacked


def scatter_direct(array, axis, dim):
    peers = lax.axis_size(axis)
    mine = lax.axis_index(axis)
    size = array.shape[dim] // peers

    def piece(owner):
        return lax.dynamic_slice_in_dim(array, owner * size, size, dim)

    total = piece(mine).astype(jnp.float32)
    for by in range(1, peers):
        sent = piece((mine + by) % peers).astype(jnp.bfloat16)
        total = total + shift(sent, axis, by).astype(jnp.float32)
    return total


def per_device(
    block_in,
    cotangent,
    block_order,
    ln1_gain,
    ln1_bias,
    w_qkv,
    b_query,
    b_value,
    w_out,
    b_out,
    ln2_gain,
    ln2_bias,
    w_up,
    b_up,
    w_down,
    b_down,
):
    inputs = block_in[0]
    row_count, width = inputs.shape
    peers = lax.axis_size("dp")
    cycle_size = lax.axis_size("ctx")
    owner_index = lax.axis_index("ctx")
    all_rows = row_count * cycle_size
    shard = width // peers

    vectors = jnp.stack(
        [ln1_gain, ln1_bias, b_query, b_value, b_out, ln2_gain, ln2_bias, b_down]
    )
    vectors = lax.all_gather(vectors, "dp", axis=0)
    qkv_full = lax.all_gather(w_qkv, "dp", axis=0, tiled=True)
    out_full = lax.all_gather(w_out, "dp", axis=0, tiled=True)
    upstream_b = cotangent[0]
    upstream_all = lax.all_gather(upstream_b, "dp", axis=0, tiled=True)

    vectors = jnp.transpose(vectors, (1, 0, 2)).reshape(8, width).astype(jnp.float32)
    gain_one, shift_one, bias_query, bias_value, bias_out, gain_two, shift_two, bias_down = [
        vectors[i] for i in range(8)
    ]

    slots = jnp.arange(all_rows, dtype=jnp.int32)
    block_rows = all_rows // block_order.shape[0]
    positions = block_order[slots // block_rows] * block_rows + slots % block_rows
    key_pos = positions[None, :]
    query_pos = lax.dynamic_slice_in_dim(positions, owner_index * row_count, row_count)[:, None]

    residual = inputs.astype(jnp.float32)
    normed_in_f, normed_one, inverse_one = norm_parts(residual, gain_one, shift_one)
    normed_in = normed_in_f.astype(jnp.bfloat16)
    projected = jnp.dot(normed_in, qkv_full, preferred_element_type=jnp.float32)
    bias_qkv = jnp.concatenate([bias_query, jnp.zeros((width,), jnp.float32), bias_value])
    projected_b = (projected + bias_qkv).astype(jnp.bfloat16)
    query_b = projected_b[:, :width]
    keys_values = gather_direct(projected_b[:, width:], "ctx").reshape(all_rows, 2 * width)
    key_all, value_all = keys_values[:, :width], keys_values[:, width:]
    attended = attend(query_pos, key_pos, query_b, key_all, value_all)

    hidden_one = (
        residual
        + jnp.dot(attended, out_full, preferred_element_type=jnp.float32)
        + bias_out
    )
    normed_mid_f, normed_two, inverse_two = norm_parts(hidden_one, gain_two, shift_two)
    normed_mid = normed_mid_f.astype(jnp.bfloat16)
    mid_all = lax.all_gather(normed_mid, "dp", axis=0, tiled=True)

    upstream = upstream_b.astype(jnp.float32)
    grad_act = contract_last(upstream_all, w_down)
    pre_act = jnp.dot(mid_all, w_up, preferred_element_type=jnp.float32) + b_up.astype(jnp.float32)
    activated = jax.nn.gelu(pre_act, approximate=False).astype(jnp.bfloat16)
    grad_pre = grad_act * gelu_slope(pre_act)
    grad_pre_b = grad_pre.astype(jnp.bfloat16)
    grad_mid = lax.psum_scatter(
        contract_last(grad_pre_b, w_up).astype(jnp.bfloat16),
        "dp",
        scatter_dimension=0,
        tiled=True,
    ).astype(jnp.float32)
    branch_out = lax.psum_scatter(
        jnp.dot(activated, w_down, preferred_element_type=jnp.float32).astype(jnp.bfloat16),
        "dp",
        scatter_dimension=0,
        tiled=True,
    ).astype(jnp.float32)
    block_out = (hidden_one + branch_out + bias_down).astype(jnp.bfloat16)

    grad_down = contract_first(activated, upstream_all)
    grad_up = contract_first(mid_all, grad_pre_b)
    grad_bias_up = jnp.sum(grad_pre, axis=0)
    g_up = scatter_direct(grad_up, "ctx", 0)
    g_down = scatter_direct(grad_down, "ctx", 1)

    grad_hidden = upstream + norm_back(grad_mid, normed_two, inverse_two, gain_two)
    grad_hidden_b = grad_hidden.astype(jnp.bfloat16)
    grad_ctx_b = contract_last(grad_hidden_b, out_full).astype(jnp.bfloat16)
    grad_query, grad_key, grad_value, query_sum, value_sum = attend_back(
        query_pos, key_pos, query_b, key_all, value_all, grad_ctx_b, attended
    )
    grad_kv = scatter_direct(jnp.concatenate([grad_key, grad_value], axis=1), "ctx", 0)
    grad_qkv = jnp.concatenate([grad_query, grad_kv.astype(jnp.bfloat16)], axis=1)

    def by_owner(left, right):
        left = left.reshape(row_count, peers, shard)
        return jnp.einsum("tnd,tc->ndc", left, right, preferred_element_type=jnp.float32).astype(
            jnp.bfloat16
        )

    out_dp = lax.psum_scatter(by_owner(attended, grad_hidden_b), "dp", scatter_dimension=0)
    qkv_dp = lax.psum_scatter(by_owner(normed_in, grad_qkv), "dp", scatter_dimension=0)
    g_out = scatter_direct(out_dp, "ctx", 1)
    g_qkv = scatter_direct(qkv_dp, "ctx", 1)

    grad_in_norm = contract_last(grad_qkv, qkv_full)
    grad_input = grad_hidden + norm_back(grad_in_norm, normed_one, inverse_one, gain_one)

    sums = jnp.stack(
        [
            jnp.sum(grad_in_norm * normed_one, axis=0),
            jnp.sum(grad_in_norm, axis=0),
            query_sum[0],
            value_sum[0],
            jnp.sum(grad_hidden, axis=0),
            jnp.sum(grad_mid * normed_two, axis=0),
            jnp.sum(grad_mid, axis=0),
            jnp.sum(upstream, axis=0),
        ]
    )
    sums = jnp.transpose(sums.reshape(8, peers, shard), (1, 0, 2))
    sums = lax.psum_scatter(sums, "dp", scatter_dimension=0)
    sums, g_bias_up = lax.psum((sums, grad_bias_up), "ctx")
    return (
        block_out[None],
        grad_input[None],
        sums[0],
        sums[1],
        g_qkv,
        sums[2],
        sums[3],
        g_out,
        sums[4],
        sums[5],
        sums[6],
        g_up,
        g_bias_up,
        g_down,
        sums[7],
    )


def solution(mesh):
    in_specs = (
        P("dp", "ctx", None),
        P("dp", "ctx", None),
        P(),
        P("dp"),
        P("dp"),
        P("dp", None),
        P("dp"),
        P("dp"),
        P("dp", None),
        P("dp"),
        P("dp"),
        P("dp"),
        P(None, "dp"),
        P("dp"),
        P("dp", None),
        P("dp"),
    )
    out_specs = (
        P("dp", "ctx", None),
        P("dp", "ctx", None),
        P("dp"),
        P("dp"),
        P("dp", "ctx"),
        P("dp"),
        P("dp"),
        P("dp", "ctx"),
        P("dp"),
        P("dp"),
        P("dp"),
        P("ctx", "dp"),
        P("dp"),
        P("dp", "ctx"),
        P("dp"),
    )
    return jax.shard_map(
        per_device, mesh=mesh, in_specs=in_specs, out_specs=out_specs, check_vma=False
    )
```

```python
import functools

import jax
import jax.numpy as jnp
from jax import lax
from jax.experimental import pallas as pl
from jax.experimental.pallas import tpu as pltpu
from jax.sharding import PartitionSpec as P

HD = 64
SCALE = 0.125


def norm_parts(values, gain_values, shift_values):
    average = jnp.mean(values, axis=-1, keepdims=True)
    centered = values - average
    inverse = lax.rsqrt(jnp.mean(centered * centered, axis=-1, keepdims=True) + 1e-05)
    normed = centered * inverse
    return normed * gain_values + shift_values, normed, inverse


def norm_back(upstream, normed, inverse, gain_values):
    scaled = upstream * gain_values
    return inverse * (
        scaled
        - jnp.mean(scaled, axis=-1, keepdims=True)
        - normed * jnp.mean(scaled * normed, axis=-1, keepdims=True)
    )


def gelu_slope(values):
    return (
        0.5 * (1.0 + lax.erf(values * 0.7071067811865476))
        + values * jnp.exp(-0.5 * values * values) * 0.3989422804014327
    )


def contract_first(left, right):
    return lax.dot_general(
        left, right, (((0,), (0,)), ((), ())), preferred_element_type=jnp.float32
    )


def contract_last(left, right):
    return lax.dot_general(
        left, right, (((1,), (1,)), ((), ())), preferred_element_type=jnp.float32
    )


def head_groups(width):
    groups = [(start, 128) for start in range(0, width - width % 128, 128)]
    if width % 128:
        groups.append((width - width % 128, width % 128))
    return groups


def head_masks(lanes):
    if lanes == HD:
        return [None]
    lane = lax.broadcasted_iota(jnp.int32, (1, lanes), 1)
    return [
        jnp.where((lane >= first) & (lane < first + HD), 1.0, 0.0).astype(jnp.bfloat16)
        for first in range(0, lanes, HD)
    ]


def keep(array, mask):
    return array if mask is None else array * mask


def visible_bias(query_pos_ref, key_pos_ref):
    return jnp.where(query_pos_ref[...] >= key_pos_ref[...], 0.0, -1e30)


def attend_kernel(query_pos_ref, key_pos_ref, q_ref, k_ref, v_ref, o_ref):
    bias = visible_bias(query_pos_ref, key_pos_ref)
    for start, lanes in head_groups(q_ref.shape[1]):
        block = slice(start, start + lanes)
        q, k, v = q_ref[:, block], k_ref[:, block], v_ref[:, block]
        total = None
        for mask in head_masks(lanes):
            scores = contract_last(keep(q, mask), k) * SCALE + bias
            largest = jnp.max(scores, axis=-1, keepdims=True)
            exponent = jnp.exp(scores - largest)
            inverse = 1.0 / jnp.sum(exponent, axis=-1, keepdims=True)
            part = (
                jnp.dot(
                    exponent.astype(jnp.bfloat16),
                    keep(v, mask),
                    preferred_element_type=jnp.float32,
                )
                * inverse
            )
            total = part if total is None else total + part
        o_ref[:, block] = total.astype(o_ref.dtype)


def attend_back_kernel(
    query_pos_ref,
    key_pos_ref,
    q_ref,
    k_ref,
    v_ref,
    do_ref,
    o_ref,
    dq_ref,
    dk_ref,
    dv_ref,
    dq_sum_ref,
    dv_sum_ref,
):
    bias = visible_bias(query_pos_ref, key_pos_ref)
    for start, lanes in head_groups(q_ref.shape[1]):
        block = slice(start, start + lanes)
        q, k, v = q_ref[:, block], k_ref[:, block], v_ref[:, block]
        do, o = do_ref[:, block], o_ref[:, block]
        product = do.astype(jnp.float32) * o.astype(jnp.float32)
        dq = dk = dv = None
        for mask in head_masks(lanes):
            q_h, k_h, do_h = keep(q, mask), keep(k, mask), keep(do, mask)
            product_h = product if mask is None else product * mask.astype(jnp.float32)
            delta = jnp.sum(product_h, axis=-1, keepdims=True)
            scores = contract_last(q_h, k) * SCALE + bias
            largest = jnp.max(scores, axis=-1, keepdims=True)
            exponent = jnp.exp(scores - largest)
            p = exponent * (1.0 / jnp.sum(exponent, axis=-1, keepdims=True))
            dp = contract_last(do_h, v)
            ds = (p * (dp - delta)).astype(jnp.bfloat16)
            dv_h = contract_first(p.astype(jnp.bfloat16), do_h)
            dq_h = jnp.dot(ds, k_h, preferred_element_type=jnp.float32)
            dk_h = contract_first(ds, q_h)
            dq = dq_h if dq is None else dq + dq_h
            dk = dk_h if dk is None else dk + dk_h
            dv = dv_h if dv is None else dv + dv_h
        dq = dq * SCALE
        dq_ref[:, block] = dq.astype(dq_ref.dtype)
        dk_ref[:, block] = (dk * SCALE).astype(dk_ref.dtype)
        dv_ref[:, block] = dv.astype(dv_ref.dtype)
        dq_sum_ref[:, block] = jnp.sum(dq, axis=0, keepdims=True)
        dv_sum_ref[:, block] = jnp.sum(dv, axis=0, keepdims=True)


def whole_vmem(count):
    return [pl.BlockSpec(memory_space=pltpu.VMEM)] * count


def attend(query_pos, key_pos, q, k, v):
    rows, width = q.shape
    keys = k.shape[0]
    return pl.pallas_call(
        attend_kernel,
        out_shape=jax.ShapeDtypeStruct((rows, width), jnp.bfloat16),
        in_specs=whole_vmem(5),
        out_specs=pl.BlockSpec(memory_space=pltpu.VMEM),
        cost_estimate=pl.CostEstimate(
            flops=8 * rows * keys * width,
            bytes_accessed=4 * (rows + keys) * width,
            transcendentals=rows * keys * (width // HD),
        ),
    )(query_pos, key_pos, q, k, v)


def attend_back(query_pos, key_pos, q, k, v, do, o):
    rows, width = q.shape
    keys = k.shape[0]
    return pl.pallas_call(
        attend_back_kernel,
        out_shape=(
            jax.ShapeDtypeStruct((rows, width), jnp.bfloat16),
            jax.ShapeDtypeStruct((keys, width), jnp.bfloat16),
            jax.ShapeDtypeStruct((keys, width), jnp.bfloat16),
            jax.ShapeDtypeStruct((1, width), jnp.float32),
            jax.ShapeDtypeStruct((1, width), jnp.float32),
        ),
        in_specs=whole_vmem(7),
        out_specs=tuple(whole_vmem(5)),
        cost_estimate=pl.CostEstimate(
            flops=20 * rows * keys * width,
            bytes_accessed=8 * (rows + keys) * width,
            transcendentals=rows * keys * (width // HD),
        ),
    )(query_pos, key_pos, q, k, v, do, o)


MESH = pl.DeviceIdType.MESH
CORES = 2
COLUMNS = 2


def place():
    index = lax.axis_index("dp")
    lines = lax.axis_size("dp") // (CORES * COLUMNS)
    core = index % CORES
    column = (index // CORES) % COLUMNS
    return index // (CORES * COLUMNS), column, core, lines


def device_at(line, column, core):
    return (line * COLUMNS + column) * CORES + core


def greet():
    line, column, core, lines = place()
    barrier = pltpu.get_barrier_semaphore()
    peers = [device_at((line + by) % lines, column, core) for by in range(1, lines)]
    peers += [device_at(line, 1 - column, core), device_at(line, column, 1 - core)]
    for peer in peers:
        pl.semaphore_signal(barrier, inc=1, device_id={"dp": peer}, device_id_type=MESH)
    pl.semaphore_wait(barrier, len(peers))


def gather_kernel(count, *refs):
    ins, outs = refs[:count], refs[count : 2 * count]
    send_sem, recv_sem, local_sem = refs[2 * count :]
    line, column, core, lines = place()
    me = device_at(line, column, core)
    greet()
    started = []

    def push(a, shard, target, way, slot, own=False):
        copy = pltpu.make_async_remote_copy(
            src_ref=ins[a] if own else outs[a].at[shard],
            dst_ref=outs[a].at[shard],
            send_sem=send_sem.at[a, way, slot],
            recv_sem=recv_sem.at[a, shard],
            device_id={"dp": target},
            device_id_type=MESH,
        )
        copy.start()
        started.append(copy)

    def arrived(a, shard):
        pltpu.make_async_remote_copy(
            src_ref=outs[a].at[shard],
            dst_ref=outs[a].at[shard],
            send_sem=send_sem.at[a, 0, 0],
            recv_sem=recv_sem.at[a, shard],
            device_id={"dp": partner},
            device_id_type=MESH,
        ).wait_recv()

    beside = device_at(line, 1 - column, core)
    partner = device_at(line, column, 1 - core)
    for a in range(count):
        push(a, me, beside, 1, 0, own=True)
        for by in range(1, lines):
            push(a, me, device_at((line + by) % lines, column, core), 0, by, own=True)
        push(a, me, partner, 2, 0, own=True)
    kept = []
    for a in range(count):
        copy = pltpu.make_async_copy(ins[a], outs[a].at[me], local_sem.at[a])
        copy.start()
        kept.append(copy)
    for a in range(count):
        for by in range(1, lines):
            shard = device_at((line - by) % lines, column, core)
            arrived(a, shard)
            push(a, shard, beside, 1, by)
            push(a, shard, partner, 2, by)
        for by in range(lines):
            shard = device_at((line - by) % lines, 1 - column, core)
            arrived(a, shard)
            push(a, shard, partner, 2, lines + by)
    for a in range(count):
        for by in range(lines):
            for across in range(COLUMNS):
                arrived(a, device_at((line - by) % lines, across, 1 - core))
    for copy in started:
        copy.wait_send()
    for copy in kept:
        copy.wait()


def gather_dp(arrays, collective_id):
    peers = lax.axis_size("dp")
    count = len(arrays)
    lines = peers // (CORES * COLUMNS)
    return pl.pallas_call(
        functools.partial(gather_kernel, count),
        out_shape=tuple(jax.ShapeDtypeStruct((peers,) + a.shape, a.dtype) for a in arrays),
        in_specs=whole_vmem(count),
        out_specs=tuple([pl.BlockSpec(memory_space=pl.ANY)] * count),
        scratch_shapes=[
            pltpu.SemaphoreType.DMA((count, 3, 2 * lines)),
            pltpu.SemaphoreType.DMA((count, peers)),
            pltpu.SemaphoreType.DMA((count,)),
        ],
        compiler_params=pltpu.CompilerParams(collective_id=collective_id, has_side_effects=True),
    )(*arrays)


def reduce_kernel(count, *refs):
    ins, outs = refs[:count], refs[count : 2 * count]
    core_bufs, side_bufs, line_bufs, side_sends, line_sends = [
        refs[(2 + i) * count : (3 + i) * count] for i in range(5)
    ]
    send_sem, recv_sem = refs[7 * count :]
    line, column, core, lines = place()
    greet()
    started = []

    def describe(a, source, landing, target, way, slot):
        return pltpu.make_async_remote_copy(
            src_ref=source,
            dst_ref=landing,
            send_sem=send_sem.at[a, way, slot],
            recv_sem=recv_sem.at[a, way, slot],
            device_id={"dp": target},
            device_id_type=MESH,
        )

    def push(*what):
        copy = describe(*what)
        copy.start()
        started.append(copy)

    def arrived(a, landing, way, slot):
        describe(a, landing, landing, partner, way, slot).wait_recv()
        return landing[...].astype(jnp.float32)

    beside = device_at(line, 1 - column, core)
    partner = device_at(line, column, 1 - core)
    order = list(range(1, lines)) + [0]
    for a in range(count):
        for slot_base, across in ((0, 1 - column), (lines, column)):
            for by in order:
                shard = device_at((line + by) % lines, across, 1 - core)
                slot = slot_base + by
                push(a, ins[a].at[shard], core_bufs[a].at[slot], partner, 0, slot)
    for a in range(count):
        for by in order:
            shard = device_at((line + by) % lines, 1 - column, core)
            total = arrived(a, core_bufs[a].at[by], 0, by) + ins[a][shard].astype(jnp.float32)
            side_sends[a][by] = total.astype(side_sends[a].dtype)
            push(a, side_sends[a].at[by], side_bufs[a].at[by], beside, 1, by)
    for a in range(count):
        for by in order:
            target = device_at((line + by) % lines, column, core)
            total = arrived(a, core_bufs[a].at[lines + by], 0, lines + by)
            total = total + ins[a][target].astype(jnp.float32)
            total = total + arrived(a, side_bufs[a].at[by], 1, by)
            if by:
                line_sends[a][by] = total.astype(line_sends[a].dtype)
                push(a, line_sends[a].at[by], line_bufs[a].at[by], target, 2, by)
            else:
                outs[a][...] = total
    for a in range(count):
        for by in range(1, lines):
            outs[a][...] += arrived(a, line_bufs[a].at[by], 2, by)
    for copy in started:
        copy.wait_send()


def reduce_dp(arrays, collective_id):
    peers = lax.axis_size("dp")
    count = len(arrays)
    lines = peers // (CORES * COLUMNS)
    buffers = []
    for size in (2 * lines, lines, lines, lines, lines):
        buffers += [pltpu.VMEM((size,) + a.shape[1:], a.dtype) for a in arrays]
    return pl.pallas_call(
        functools.partial(reduce_kernel, count),
        out_shape=tuple(jax.ShapeDtypeStruct(a.shape[1:], jnp.float32) for a in arrays),
        in_specs=whole_vmem(count),
        out_specs=tuple(whole_vmem(count)),
        scratch_shapes=buffers
        + [
            pltpu.SemaphoreType.DMA((count, 3, 2 * lines)),
            pltpu.SemaphoreType.DMA((count, 3, 2 * lines)),
        ],
        compiler_params=pltpu.CompilerParams(collective_id=collective_id, has_side_effects=True),
    )(*arrays)


def shift(array, axis, by):
    peers = lax.axis_size(axis)
    return lax.ppermute(array, axis, [(i, (i + by) % peers) for i in range(peers)])


def gather_direct(array, axis):
    peers = lax.axis_size(axis)
    mine = lax.axis_index(axis)
    held = [array] + [shift(array, axis, by) for by in range(1, peers)]
    stacked = jnp.zeros((peers,) + array.shape, array.dtype)
    for by in range(peers):
        stacked = lax.dynamic_update_index_in_dim(stacked, held[by], (mine - by) % peers, 0)
    return stacked


def scatter_direct(array, axis, dim):
    peers = lax.axis_size(axis)
    mine = lax.axis_index(axis)
    size = array.shape[dim] // peers

    def piece(owner):
        return lax.dynamic_slice_in_dim(array, owner * size, size, dim)

    total = piece(mine).astype(jnp.float32)
    for by in range(1, peers):
        sent = piece((mine + by) % peers).astype(jnp.bfloat16)
        total = total + shift(sent, axis, by).astype(jnp.float32)
    return total


def per_device(
    block_in,
    cotangent,
    block_order,
    ln1_gain,
    ln1_bias,
    w_qkv,
    b_query,
    b_value,
    w_out,
    b_out,
    ln2_gain,
    ln2_bias,
    w_up,
    b_up,
    w_down,
    b_down,
):
    inputs = block_in[0]
    row_count, width = inputs.shape
    peers = lax.axis_size("dp")
    cycle_size = lax.axis_size("ctx")
    owner_index = lax.axis_index("ctx")
    all_rows = row_count * cycle_size
    shard = width // peers

    vectors = jnp.stack(
        [ln1_gain, ln1_bias, b_query, b_value, b_out, ln2_gain, ln2_bias, b_down]
    )
    vectors, qkv_full, out_full = gather_dp([vectors, w_qkv, w_out], 0)
    qkv_full = qkv_full.reshape(width, 3 * width)
    out_full = out_full.reshape(width, width)
    upstream_b = cotangent[0]

    vectors = jnp.transpose(vectors, (1, 0, 2)).reshape(8, width).astype(jnp.float32)
    gain_one, shift_one, bias_query, bias_value, bias_out, gain_two, shift_two, bias_down = [
        vectors[i] for i in range(8)
    ]

    slots = jnp.arange(all_rows, dtype=jnp.int32)
    block_rows = all_rows // block_order.shape[0]
    positions = block_order[slots // block_rows] * block_rows + slots % block_rows
    key_pos = positions[None, :]
    query_pos = lax.dynamic_slice_in_dim(positions, owner_index * row_count, row_count)[:, None]

    residual = inputs.astype(jnp.float32)
    normed_in_f, normed_one, inverse_one = norm_parts(residual, gain_one, shift_one)
    normed_in = normed_in_f.astype(jnp.bfloat16)
    projected = jnp.dot(normed_in, qkv_full, preferred_element_type=jnp.float32)
    bias_qkv = jnp.concatenate([bias_query, jnp.zeros((width,), jnp.float32), bias_value])
    projected_b = (projected + bias_qkv).astype(jnp.bfloat16)
    query_b = projected_b[:, :width]
    keys_values = gather_direct(projected_b[:, width:], "ctx").reshape(all_rows, 2 * width)
    key_all, value_all = keys_values[:, :width], keys_values[:, width:]
    attended = attend(query_pos, key_pos, query_b, key_all, value_all)

    hidden_one = (
        residual
        + jnp.dot(attended, out_full, preferred_element_type=jnp.float32)
        + bias_out
    )
    normed_mid_f, normed_two, inverse_two = norm_parts(hidden_one, gain_two, shift_two)
    normed_mid = normed_mid_f.astype(jnp.bfloat16)
    mid_all, upstream_all = gather_dp([normed_mid, upstream_b], 1)
    mid_all = mid_all.reshape(peers * row_count, width)
    upstream_all = upstream_all.reshape(peers * row_count, width)

    upstream = upstream_b.astype(jnp.float32)
    grad_act = contract_last(upstream_all, w_down)
    pre_act = jnp.dot(mid_all, w_up, preferred_element_type=jnp.float32) + b_up.astype(jnp.float32)
    activated = jax.nn.gelu(pre_act, approximate=False).astype(jnp.bfloat16)
    grad_pre = grad_act * gelu_slope(pre_act)
    grad_pre_b = grad_pre.astype(jnp.bfloat16)
    grad_mid, branch_out = reduce_dp(
        [
            part.astype(jnp.bfloat16).reshape(peers, row_count, width)
            for part in (
                contract_last(grad_pre_b, w_up),
                jnp.dot(activated, w_down, preferred_element_type=jnp.float32),
            )
        ],
        2,
    )
    block_out = (hidden_one + branch_out + bias_down).astype(jnp.bfloat16)

    grad_down = contract_first(activated, upstream_all)
    grad_up = contract_first(mid_all, grad_pre_b)
    grad_bias_up = jnp.sum(grad_pre, axis=0)
    g_up = scatter_direct(grad_up, "ctx", 0)
    g_down = scatter_direct(grad_down, "ctx", 1)

    grad_hidden = upstream + norm_back(grad_mid, normed_two, inverse_two, gain_two)
    grad_hidden_b = grad_hidden.astype(jnp.bfloat16)
    grad_ctx_b = contract_last(grad_hidden_b, out_full).astype(jnp.bfloat16)
    grad_query, grad_key, grad_value, query_sum, value_sum = attend_back(
        query_pos, key_pos, query_b, key_all, value_all, grad_ctx_b, attended
    )
    grad_kv = scatter_direct(jnp.concatenate([grad_key, grad_value], axis=1), "ctx", 0)
    grad_qkv = jnp.concatenate([grad_query, grad_kv.astype(jnp.bfloat16)], axis=1)

    def by_owner(left, right):
        left = left.reshape(row_count, peers, shard)
        return jnp.einsum("tnd,tc->ndc", left, right, preferred_element_type=jnp.float32).astype(
            jnp.bfloat16
        )

    grad_in_norm = contract_last(grad_qkv, qkv_full)
    grad_input = grad_hidden + norm_back(grad_in_norm, normed_one, inverse_one, gain_one)

    sums = jnp.stack(
        [
            jnp.sum(grad_in_norm * normed_one, axis=0),
            jnp.sum(grad_in_norm, axis=0),
            query_sum[0],
            value_sum[0],
            jnp.sum(grad_hidden, axis=0),
            jnp.sum(grad_mid * normed_two, axis=0),
            jnp.sum(grad_mid, axis=0),
            jnp.sum(upstream, axis=0),
        ]
    )
    sums = jnp.transpose(sums.reshape(8, peers, shard), (1, 0, 2))
    qkv_dp, out_dp, sums = reduce_dp(
        [by_owner(normed_in, grad_qkv), by_owner(attended, grad_hidden_b), sums], 3
    )
    g_out = scatter_direct(out_dp, "ctx", 1)
    g_qkv = scatter_direct(qkv_dp, "ctx", 1)
    sums, g_bias_up = lax.psum((sums, grad_bias_up), "ctx")
    return (
        block_out[None],
        grad_input[None],
        sums[0],
        sums[1],
        g_qkv,
        sums[2],
        sums[3],
        g_out,
        sums[4],
        sums[5],
        sums[6],
        g_up,
        g_bias_up,
        g_down,
        sums[7],
    )


def solution(mesh):
    in_specs = (
        P("dp", "ctx", None),
        P("dp", "ctx", None),
        P(),
        P("dp"),
        P("dp"),
        P("dp", None),
        P("dp"),
        P("dp"),
        P("dp", None),
        P("dp"),
        P("dp"),
        P("dp"),
        P(None, "dp"),
        P("dp"),
        P("dp", None),
        P("dp"),
    )
    out_specs = (
        P("dp", "ctx", None),
        P("dp", "ctx", None),
        P("dp"),
        P("dp"),
        P("dp", "ctx"),
        P("dp"),
        P("dp"),
        P("dp", "ctx"),
        P("dp"),
        P("dp"),
        P("dp"),
        P("ctx", "dp"),
        P("dp"),
        P("dp", "ctx"),
        P("dp"),
    )
    return jax.shard_map(
        per_device, mesh=mesh, in_specs=in_specs, out_specs=out_specs, check_vma=False
    )
```

```python
import functools

import jax
import jax.numpy as jnp
from jax import lax
from jax.experimental import pallas as pl
from jax.experimental.pallas import tpu as pltpu
from jax.sharding import PartitionSpec as P

HD = 64
SCALE = 0.125


def norm_parts(values, gain_values, shift_values):
    average = jnp.mean(values, axis=-1, keepdims=True)
    centered = values - average
    inverse = lax.rsqrt(jnp.mean(centered * centered, axis=-1, keepdims=True) + 1e-05)
    normed = centered * inverse
    return normed * gain_values + shift_values, normed, inverse


def norm_back(upstream, normed, inverse, gain_values):
    scaled = upstream * gain_values
    return inverse * (
        scaled
        - jnp.mean(scaled, axis=-1, keepdims=True)
        - normed * jnp.mean(scaled * normed, axis=-1, keepdims=True)
    )


def gelu_slope(values):
    return (
        0.5 * (1.0 + lax.erf(values * 0.7071067811865476))
        + values * jnp.exp(-0.5 * values * values) * 0.3989422804014327
    )


def contract_first(left, right):
    return lax.dot_general(
        left, right, (((0,), (0,)), ((), ())), preferred_element_type=jnp.float32
    )


def contract_last(left, right):
    return lax.dot_general(
        left, right, (((1,), (1,)), ((), ())), preferred_element_type=jnp.float32
    )


def head_groups(width):
    groups = [(start, 128) for start in range(0, width - width % 128, 128)]
    if width % 128:
        groups.append((width - width % 128, width % 128))
    return groups


def head_masks(lanes):
    if lanes == HD:
        return [None]
    lane = lax.broadcasted_iota(jnp.int32, (1, lanes), 1)
    return [
        jnp.where((lane >= first) & (lane < first + HD), 1.0, 0.0).astype(jnp.bfloat16)
        for first in range(0, lanes, HD)
    ]


def keep(array, mask):
    return array if mask is None else array * mask


def visible_bias(query_pos_ref, key_pos_ref):
    return jnp.where(query_pos_ref[...] >= key_pos_ref[...], 0.0, -1e30)


def attend_kernel(query_pos_ref, key_pos_ref, q_ref, k_ref, v_ref, o_ref):
    bias = visible_bias(query_pos_ref, key_pos_ref)
    for start, lanes in head_groups(q_ref.shape[1]):
        block = slice(start, start + lanes)
        q, k, v = q_ref[:, block], k_ref[:, block], v_ref[:, block]
        total = None
        for mask in head_masks(lanes):
            scores = contract_last(keep(q, mask), k) * SCALE + bias
            largest = jnp.max(scores, axis=-1, keepdims=True)
            exponent = jnp.exp(scores - largest)
            inverse = 1.0 / jnp.sum(exponent, axis=-1, keepdims=True)
            part = (
                jnp.dot(
                    exponent.astype(jnp.bfloat16),
                    keep(v, mask),
                    preferred_element_type=jnp.float32,
                )
                * inverse
            )
            total = part if total is None else total + part
        o_ref[:, block] = total.astype(o_ref.dtype)


def attend_back_kernel(
    query_pos_ref,
    key_pos_ref,
    q_ref,
    k_ref,
    v_ref,
    do_ref,
    o_ref,
    dq_ref,
    dk_ref,
    dv_ref,
    dq_sum_ref,
    dv_sum_ref,
):
    bias = visible_bias(query_pos_ref, key_pos_ref)
    for start, lanes in head_groups(q_ref.shape[1]):
        block = slice(start, start + lanes)
        q, k, v = q_ref[:, block], k_ref[:, block], v_ref[:, block]
        do, o = do_ref[:, block], o_ref[:, block]
        product = do.astype(jnp.float32) * o.astype(jnp.float32)
        dq = dk = dv = None
        for mask in head_masks(lanes):
            q_h, k_h, do_h = keep(q, mask), keep(k, mask), keep(do, mask)
            product_h = product if mask is None else product * mask.astype(jnp.float32)
            delta = jnp.sum(product_h, axis=-1, keepdims=True)
            scores = contract_last(q_h, k) * SCALE + bias
            largest = jnp.max(scores, axis=-1, keepdims=True)
            exponent = jnp.exp(scores - largest)
            p = exponent * (1.0 / jnp.sum(exponent, axis=-1, keepdims=True))
            dp = contract_last(do_h, v)
            ds = (p * (dp - delta)).astype(jnp.bfloat16)
            dv_h = contract_first(p.astype(jnp.bfloat16), do_h)
            dq_h = jnp.dot(ds, k_h, preferred_element_type=jnp.float32)
            dk_h = contract_first(ds, q_h)
            dq = dq_h if dq is None else dq + dq_h
            dk = dk_h if dk is None else dk + dk_h
            dv = dv_h if dv is None else dv + dv_h
        dq = dq * SCALE
        dq_ref[:, block] = dq.astype(dq_ref.dtype)
        dk_ref[:, block] = (dk * SCALE).astype(dk_ref.dtype)
        dv_ref[:, block] = dv.astype(dv_ref.dtype)
        dq_sum_ref[:, block] = jnp.sum(dq, axis=0, keepdims=True)
        dv_sum_ref[:, block] = jnp.sum(dv, axis=0, keepdims=True)


def whole_vmem(count):
    return [pl.BlockSpec(memory_space=pltpu.VMEM)] * count


def attend(query_pos, key_pos, q, k, v):
    rows, width = q.shape
    keys = k.shape[0]
    return pl.pallas_call(
        attend_kernel,
        out_shape=jax.ShapeDtypeStruct((rows, width), jnp.bfloat16),
        in_specs=whole_vmem(5),
        out_specs=pl.BlockSpec(memory_space=pltpu.VMEM),
        cost_estimate=pl.CostEstimate(
            flops=8 * rows * keys * width,
            bytes_accessed=4 * (rows + keys) * width,
            transcendentals=rows * keys * (width // HD),
        ),
    )(query_pos, key_pos, q, k, v)


def attend_back(query_pos, key_pos, q, k, v, do, o):
    rows, width = q.shape
    keys = k.shape[0]
    return pl.pallas_call(
        attend_back_kernel,
        out_shape=(
            jax.ShapeDtypeStruct((rows, width), jnp.bfloat16),
            jax.ShapeDtypeStruct((keys, width), jnp.bfloat16),
            jax.ShapeDtypeStruct((keys, width), jnp.bfloat16),
            jax.ShapeDtypeStruct((1, width), jnp.float32),
            jax.ShapeDtypeStruct((1, width), jnp.float32),
        ),
        in_specs=whole_vmem(7),
        out_specs=tuple(whole_vmem(5)),
        cost_estimate=pl.CostEstimate(
            flops=20 * rows * keys * width,
            bytes_accessed=8 * (rows + keys) * width,
            transcendentals=rows * keys * (width // HD),
        ),
    )(query_pos, key_pos, q, k, v, do, o)


MESH = pl.DeviceIdType.MESH
CORES = 2
COLUMNS = 2
SIDES = ((1, 2), (-1, 3))


def place():
    index = lax.axis_index("dp")
    lines = lax.axis_size("dp") // (CORES * COLUMNS)
    core = index % CORES
    column = (index // CORES) % COLUMNS
    return index // (CORES * COLUMNS), column, core, lines


def device_at(line, column, core):
    return (line * COLUMNS + column) * CORES + core


def on_line(line, lines):
    return (line >= 0) & (line < lines)


def greet():
    line, column, core, lines = place()
    barrier = pltpu.get_barrier_semaphore()
    peers = [device_at((line + by) % lines, column, core) for by in range(1, lines)]
    peers += [device_at(line, 1 - column, core), device_at(line, column, 1 - core)]
    for peer in peers:
        pl.semaphore_signal(barrier, inc=1, device_id={"dp": peer}, device_id_type=MESH)
    pl.semaphore_wait(barrier, len(peers))


def gather_kernel(count, *refs):
    ins, outs = refs[:count], refs[count : 2 * count]
    send_sem, recv_sem, local_sem = refs[2 * count :]
    line, column, core, lines = place()
    me = device_at(line, column, core)
    greet()

    def describe(a, shard, target, way, slot, own=False):
        return pltpu.make_async_remote_copy(
            src_ref=ins[a] if own else outs[a].at[shard],
            dst_ref=outs[a].at[shard],
            send_sem=send_sem.at[a, way, slot],
            recv_sem=recv_sem.at[a, shard],
            device_id={"dp": target},
            device_id_type=MESH,
        )

    def push(*what, own=False):
        describe(*what, own=own).start()

    def arrived(a, shard):
        describe(a, shard, partner, 0, 0).wait_recv()

    def sent(a, way, slot):
        describe(a, me, partner, way, slot).wait_send()

    beside = device_at(line, 1 - column, core)
    partner = device_at(line, column, 1 - core)

    def along(step):
        return device_at(line + step, column, core)

    for a in range(count):
        push(a, me, beside, 1, 0, own=True)
        for step, way in SIDES:

            @pl.when(on_line(line + step, lines))
            def _():
                push(a, me, along(step), way, 0, own=True)

        push(a, me, partner, 4, 0, own=True)
    for a in range(count):
        pltpu.make_async_copy(ins[a], outs[a].at[me], local_sem.at[a]).start()
    for by in range(1, lines):
        for a in range(count):
            for step, way in SIDES:

                @pl.when(on_line(line - step * by, lines))
                def _():
                    shard = along(-step * by)
                    arrived(a, shard)

                    @pl.when(on_line(line + step, lines))
                    def _():
                        push(a, shard, along(step), way, by)

                    push(a, shard, beside, 1, lines + step * by)
                    push(a, shard, partner, 4, lines + step * by)

    for a in range(count):
        arrived(a, device_at(line, 1 - column, core))
        push(a, device_at(line, 1 - column, core), partner, 4, 2 * lines)
    for by in range(1, lines):
        for a in range(count):
            for step, _ in SIDES:

                @pl.when(on_line(line - step * by, lines))
                def _():
                    shard = device_at(line - step * by, 1 - column, core)
                    arrived(a, shard)
                    push(a, shard, partner, 4, 3 * lines + step * by)

    for a in range(count):
        for by in range(lines):
            for across in range(COLUMNS):
                arrived(a, device_at(by, across, 1 - core))
    for a in range(count):
        sent(a, 1, 0)
        sent(a, 4, 0)
        sent(a, 4, 2 * lines)
        for step, way in SIDES:

            @pl.when(on_line(line + step, lines))
            def _():
                sent(a, way, 0)

            for by in range(1, lines):

                @pl.when(on_line(line - step * by, lines))
                def _():
                    @pl.when(on_line(line + step, lines))
                    def _():
                        sent(a, way, by)

                    sent(a, 1, lines + step * by)
                    sent(a, 4, lines + step * by)
                    sent(a, 4, 3 * lines + step * by)

        pltpu.make_async_copy(ins[a], outs[a].at[me], local_sem.at[a]).wait()


def gather_dp(arrays, collective_id):
    peers = lax.axis_size("dp")
    count = len(arrays)
    lines = peers // (CORES * COLUMNS)
    return pl.pallas_call(
        functools.partial(gather_kernel, count),
        out_shape=tuple(jax.ShapeDtypeStruct((peers,) + a.shape, a.dtype) for a in arrays),
        in_specs=whole_vmem(count),
        out_specs=tuple([pl.BlockSpec(memory_space=pl.ANY)] * count),
        scratch_shapes=[
            pltpu.SemaphoreType.DMA((count, 5, 4 * lines)),
            pltpu.SemaphoreType.DMA((count, peers)),
            pltpu.SemaphoreType.DMA((count,)),
        ],
        compiler_params=pltpu.CompilerParams(collective_id=collective_id, has_side_effects=True),
    )(*arrays)


def reduce_kernel(count, *refs):
    ins, outs = refs[:count], refs[count : 2 * count]
    core_bufs, side_bufs, up_bufs, down_bufs, side_sends, line_sends = [
        refs[(2 + i) * count : (3 + i) * count] for i in range(6)
    ]
    send_sem, recv_sem = refs[8 * count :]
    line, column, core, lines = place()
    beside = device_at(line, 1 - column, core)
    partner = device_at(line, column, 1 - core)
    greet()

    def describe(a, source, landing, target, way, slot):
        return pltpu.make_async_remote_copy(
            src_ref=source,
            dst_ref=landing,
            send_sem=send_sem.at[a, way, slot],
            recv_sem=recv_sem.at[a, way, slot],
            device_id={"dp": target},
            device_id_type=MESH,
        )

    def arrived(a, landing, way, slot):
        describe(a, landing, landing, partner, way, slot).wait_recv()
        return landing[...].astype(jnp.float32)

    def for_lines(visit):
        for by in range(lines - 1, 0, -1):
            for a in range(count):
                for step, _ in SIDES:

                    @pl.when(on_line(line + step * by, lines))
                    def _():
                        visit(a, line + step * by, step, by)

        for a in range(count):
            visit(a, line, 0, 0)

    def to_partner(across):
        def visit(a, target, step, by):
            slot = target if across is beside else lines + target
            shard = device_at(target, 1 - column if across is beside else column, 1 - core)
            describe(a, ins[a].at[shard], core_bufs[a].at[slot], partner, 0, slot).start()

        return visit

    def to_beside(a, target, step, by):
        total = arrived(a, core_bufs[a].at[target], 0, target)
        total = total + ins[a][device_at(target, 1 - column, core)].astype(jnp.float32)
        side_sends[a][target] = total.astype(side_sends[a].dtype)
        describe(
            a, side_sends[a].at[target], side_bufs[a].at[target], beside, 1, target
        ).start()

    def along(a, target, step, by):
        total = arrived(a, core_bufs[a].at[lines + target], 0, lines + target)
        total = total + ins[a][device_at(target, column, core)].astype(jnp.float32)
        total = total + arrived(a, side_bufs[a].at[target], 1, target)
        if step == 0:
            outs[a][...] = total
        else:
            way, landing = (2, up_bufs[a]) if step > 0 else (3, down_bufs[a])
            line_sends[a][target] = total.astype(line_sends[a].dtype)

            @pl.when(on_line(line - step, lines))
            def _():
                more = arrived(a, landing.at[target], way, target)
                line_sends[a][target] = (total + more).astype(line_sends[a].dtype)

            describe(
                a,
                line_sends[a].at[target],
                landing.at[target],
                device_at(line + step, column, core),
                way,
                target,
            ).start()

    for_lines(to_partner(beside))
    for_lines(to_partner(None))
    for_lines(to_beside)
    for_lines(along)
    for a in range(count):
        for step, way, landing in ((1, 2, up_bufs[a]), (-1, 3, down_bufs[a])):

            @pl.when(on_line(line - step, lines))
            def _():
                outs[a][...] += arrived(a, landing.at[line], way, line)

    def sent(a, target, step, by):
        buffer = line_sends[a].at[target]
        describe(a, buffer, buffer, partner, 0, target).wait_send()
        describe(a, buffer, buffer, partner, 0, lines + target).wait_send()
        describe(a, buffer, buffer, partner, 1, target).wait_send()
        if step:
            describe(a, buffer, buffer, partner, 2 if step > 0 else 3, target).wait_send()

    for_lines(sent)


def reduce_dp(arrays, collective_id):
    peers = lax.axis_size("dp")
    count = len(arrays)
    lines = peers // (CORES * COLUMNS)
    buffers = []
    for size in (2 * lines, lines, lines, lines, lines, lines):
        buffers += [pltpu.VMEM((size,) + a.shape[1:], a.dtype) for a in arrays]
    return pl.pallas_call(
        functools.partial(reduce_kernel, count),
        out_shape=tuple(jax.ShapeDtypeStruct(a.shape[1:], jnp.float32) for a in arrays),
        in_specs=whole_vmem(count),
        out_specs=tuple(whole_vmem(count)),
        scratch_shapes=buffers
        + [
            pltpu.SemaphoreType.DMA((count, 4, 2 * lines)),
            pltpu.SemaphoreType.DMA((count, 4, 2 * lines)),
        ],
        compiler_params=pltpu.CompilerParams(collective_id=collective_id, has_side_effects=True),
    )(*arrays)


def shift(array, axis, by):
    peers = lax.axis_size(axis)
    return lax.ppermute(array, axis, [(i, (i + by) % peers) for i in range(peers)])


def gather_direct(array, axis):
    peers = lax.axis_size(axis)
    mine = lax.axis_index(axis)
    held = [array] + [shift(array, axis, by) for by in range(1, peers)]
    stacked = jnp.zeros((peers,) + array.shape, array.dtype)
    for by in range(peers):
        stacked = lax.dynamic_update_index_in_dim(stacked, held[by], (mine - by) % peers, 0)
    return stacked


def scatter_direct(array, axis, dim):
    peers = lax.axis_size(axis)
    mine = lax.axis_index(axis)
    size = array.shape[dim] // peers

    def piece(owner):
        return lax.dynamic_slice_in_dim(array, owner * size, size, dim)

    total = piece(mine).astype(jnp.float32)
    for by in range(1, peers):
        sent = piece((mine + by) % peers).astype(jnp.bfloat16)
        total = total + shift(sent, axis, by).astype(jnp.float32)
    return total


def per_device(
    block_in,
    cotangent,
    block_order,
    ln1_gain,
    ln1_bias,
    w_qkv,
    b_query,
    b_value,
    w_out,
    b_out,
    ln2_gain,
    ln2_bias,
    w_up,
    b_up,
    w_down,
    b_down,
):
    inputs = block_in[0]
    row_count, width = inputs.shape
    peers = lax.axis_size("dp")
    cycle_size = lax.axis_size("ctx")
    owner_index = lax.axis_index("ctx")
    all_rows = row_count * cycle_size
    shard = width // peers

    vectors = jnp.stack(
        [ln1_gain, ln1_bias, b_query, b_value, b_out, ln2_gain, ln2_bias, b_down]
    )
    vectors, qkv_full, out_full = gather_dp([vectors, w_qkv, w_out], 0)
    qkv_full = qkv_full.reshape(width, 3 * width)
    out_full = out_full.reshape(width, width)
    upstream_b = cotangent[0]

    vectors = jnp.transpose(vectors, (1, 0, 2)).reshape(8, width).astype(jnp.float32)
    gain_one, shift_one, bias_query, bias_value, bias_out, gain_two, shift_two, bias_down = [
        vectors[i] for i in range(8)
    ]

    slots = jnp.arange(all_rows, dtype=jnp.int32)
    block_rows = all_rows // block_order.shape[0]
    positions = block_order[slots // block_rows] * block_rows + slots % block_rows
    key_pos = positions[None, :]
    query_pos = lax.dynamic_slice_in_dim(positions, owner_index * row_count, row_count)[:, None]

    residual = inputs.astype(jnp.float32)
    normed_in_f, normed_one, inverse_one = norm_parts(residual, gain_one, shift_one)
    normed_in = normed_in_f.astype(jnp.bfloat16)
    projected = jnp.dot(normed_in, qkv_full, preferred_element_type=jnp.float32)
    bias_qkv = jnp.concatenate([bias_query, jnp.zeros((width,), jnp.float32), bias_value])
    projected_b = (projected + bias_qkv).astype(jnp.bfloat16)
    query_b = projected_b[:, :width]
    keys_values = gather_direct(projected_b[:, width:], "ctx").reshape(all_rows, 2 * width)
    key_all, value_all = keys_values[:, :width], keys_values[:, width:]
    attended = attend(query_pos, key_pos, query_b, key_all, value_all)

    hidden_one = (
        residual
        + jnp.dot(attended, out_full, preferred_element_type=jnp.float32)
        + bias_out
    )
    normed_mid_f, normed_two, inverse_two = norm_parts(hidden_one, gain_two, shift_two)
    normed_mid = normed_mid_f.astype(jnp.bfloat16)
    mid_all, upstream_all = gather_dp([normed_mid, upstream_b], 1)
    mid_all = mid_all.reshape(peers * row_count, width)
    upstream_all = upstream_all.reshape(peers * row_count, width)

    upstream = upstream_b.astype(jnp.float32)
    grad_act = contract_last(upstream_all, w_down)
    pre_act = jnp.dot(mid_all, w_up, preferred_element_type=jnp.float32) + b_up.astype(jnp.float32)
    activated = jax.nn.gelu(pre_act, approximate=False).astype(jnp.bfloat16)
    grad_pre = grad_act * gelu_slope(pre_act)
    grad_pre_b = grad_pre.astype(jnp.bfloat16)
    grad_mid, branch_out = reduce_dp(
        [
            part.astype(jnp.bfloat16).reshape(peers, row_count, width)
            for part in (
                contract_last(grad_pre_b, w_up),
                jnp.dot(activated, w_down, preferred_element_type=jnp.float32),
            )
        ],
        2,
    )
    block_out = (hidden_one + branch_out + bias_down).astype(jnp.bfloat16)

    grad_down = contract_first(activated, upstream_all)
    grad_up = contract_first(mid_all, grad_pre_b)
    grad_bias_up = jnp.sum(grad_pre, axis=0)
    g_up = scatter_direct(grad_up, "ctx", 0)
    g_down = scatter_direct(grad_down, "ctx", 1)

    grad_hidden = upstream + norm_back(grad_mid, normed_two, inverse_two, gain_two)
    grad_hidden_b = grad_hidden.astype(jnp.bfloat16)
    grad_ctx_b = contract_last(grad_hidden_b, out_full).astype(jnp.bfloat16)
    grad_query, grad_key, grad_value, query_sum, value_sum = attend_back(
        query_pos, key_pos, query_b, key_all, value_all, grad_ctx_b, attended
    )
    grad_kv = scatter_direct(jnp.concatenate([grad_key, grad_value], axis=1), "ctx", 0)
    grad_qkv = jnp.concatenate([grad_query, grad_kv.astype(jnp.bfloat16)], axis=1)

    def by_owner(left, right):
        left = left.reshape(row_count, peers, shard)
        return jnp.einsum("tnd,tc->ndc", left, right, preferred_element_type=jnp.float32).astype(
            jnp.bfloat16
        )

    grad_in_norm = contract_last(grad_qkv, qkv_full)
    grad_input = grad_hidden + norm_back(grad_in_norm, normed_one, inverse_one, gain_one)

    sums = jnp.stack(
        [
            jnp.sum(grad_in_norm * normed_one, axis=0),
            jnp.sum(grad_in_norm, axis=0),
            query_sum[0],
            value_sum[0],
            jnp.sum(grad_hidden, axis=0),
            jnp.sum(grad_mid * normed_two, axis=0),
            jnp.sum(grad_mid, axis=0),
            jnp.sum(upstream, axis=0),
        ]
    )
    sums = jnp.transpose(sums.reshape(8, peers, shard), (1, 0, 2))
    qkv_dp, out_dp, sums = reduce_dp(
        [by_owner(normed_in, grad_qkv), by_owner(attended, grad_hidden_b), sums], 3
    )
    g_out = scatter_direct(out_dp, "ctx", 1)
    g_qkv = scatter_direct(qkv_dp, "ctx", 1)
    sums = jnp.sum(gather_direct(sums, "ctx"), axis=0)
    g_bias_up = jnp.sum(gather_direct(grad_bias_up, "ctx"), axis=0)
    return (
        block_out[None],
        grad_input[None],
        sums[0],
        sums[1],
        g_qkv,
        sums[2],
        sums[3],
        g_out,
        sums[4],
        sums[5],
        sums[6],
        g_up,
        g_bias_up,
        g_down,
        sums[7],
    )


def solution(mesh):
    in_specs = (
        P("dp", "ctx", None),
        P("dp", "ctx", None),
        P(),
        P("dp"),
        P("dp"),
        P("dp", None),
        P("dp"),
        P("dp"),
        P("dp", None),
        P("dp"),
        P("dp"),
        P("dp"),
        P(None, "dp"),
        P("dp"),
        P("dp", None),
        P("dp"),
    )
    out_specs = (
        P("dp", "ctx", None),
        P("dp", "ctx", None),
        P("dp"),
        P("dp"),
        P("dp", "ctx"),
        P("dp"),
        P("dp"),
        P("dp", "ctx"),
        P("dp"),
        P("dp"),
        P("dp"),
        P("ctx", "dp"),
        P("dp"),
        P("dp", "ctx"),
        P("dp"),
    )
    return jax.shard_map(
        per_device, mesh=mesh, in_specs=in_specs, out_specs=out_specs, check_vma=False
    )
```
